512 devices in a mesh: rows: 512 (over z, x, y, core).
Axes of the slice: x: 4, y: 4, z: 16, core: 2. Of those that a mesh axis runs over, the one named last changes fastest.
Arguments:
- signal: bfloat16 [524288, 256], P('rows'), may hold values from -6 to 6
- leaves: bfloat16 [524288, 512], P('rows'), may hold values from -0.25 to 0.25
- bases: bfloat16 [4, 524288, 128], P(None, 'rows'), may hold values from -6 to 6
- couplings: bfloat16 [15, 128, 128], replicated, may hold values from -0.5 to 0.5
- weights: float32 [524288], P('rows'), may hold values from 0.25 to 4
Outputs:
- result: bfloat16 [524288, 256], P('rows')
The draws below stay inside these ranges and needn't reach their ends.
All inputs are finite; a program needn't handle non-finite values.
Results may differ from the reference program's by a relative error of at most 0.007.
Values sent between devices are 32-bit elements; how exact they have to be, the bound alone decides.
A program may use at most 64 MiB of HBM per device.

```python
import math
import jax
import jax.numpy as jnp
from jax import lax

NRHS = 256
LEAF = 512
R = 128
LEVELS = 4
N = 524288


def block_levels(rng, shape, shards, low, top_value):
    factor_of = 1.0
    for dim, shards_of in shards:
        draws = jax.random.uniform(jax.random.fold_in(jax.random.fold_in(rng, 6), dim), (shards_of,), jnp.float32, low / len(shards), top_value / len(shards))
        factor_of = factor_of * jnp.repeat(jnp.exp(draws), shape[dim] // shards_of).reshape((-1,) + (1,) * (len(shape) - 1 - dim))
    return factor_of


def scatter_about(stream_key, dims, scale, most, cuts=(), kind=jnp.bfloat16):
    values = jax.random.normal(stream_key, dims, jnp.float32) * scale
    if len(cuts) > 0:
        values = block_levels(stream_key, dims, cuts, -0.22, 0.18) * values
    return jnp.clip(values, min=-most, max=most).astype(kind)


def setup_inputs(seed: int = 0) -> dict:
    arg_keys = jax.random.split(jax.random.key(seed), 6)
    signal = scatter_about(arg_keys[0], (N, NRHS), 1.0, 6.0, ((0, 512),))
    leaves = scatter_about(arg_keys[1], (N, LEAF), LEAF ** -0.5, 0.25, ((0, 512),))
    bases = scatter_about(arg_keys[2], (LEVELS, N, R), 1.0, 6.0, ((1, 512),))
    couplings = scatter_about(arg_keys[3], (2 ** LEVELS - 1, R, R), R ** -0.5, 0.5)
    weights = jnp.clip(jnp.exp(math.log(4.0) - 2.7725887 * jax.random.uniform(arg_keys[4], (N,), jnp.float32) ** block_levels(arg_keys[4], (N,), ((0, 512),), -0.2, 0.2)), 0.25, 4.0)
    return dict(signal=signal, leaves=leaves, bases=bases, couplings=couplings, weights=weights)


def kernel_apply(vec, leaves, bases, couplings):
    total = vec.shape[0]
    width = vec.shape[1]
    count = total // LEAF
    blocks = leaves.reshape(count, LEAF, LEAF)
    parts = vec.reshape(count, LEAF, width)
    leaf_out = lax.map(lambda pair: jnp.dot(pair[0], pair[1], preferred_element_type=jnp.float32), (blocks, parts))
    result = leaf_out.reshape(total, width)
    for level in range(LEVELS):
        nodes = 2 ** (level + 1)
        size = total // nodes
        factor = 1.0 / math.sqrt(size * R)
        node_bases = bases[level].reshape(nodes, size, R)
        node_vecs = vec.reshape(nodes, size, width)
        proj = [jnp.dot(node_bases[k].T, node_vecs[k], preferred_element_type=jnp.float32) for k in range(nodes)]
        pieces = []
        for pair_idx in range(nodes // 2):
            coupling = couplings[nodes // 2 - 1 + pair_idx]
            left_q = (proj[2 * pair_idx + 1] * factor).astype(jnp.bfloat16)
            right_q = (proj[2 * pair_idx] * factor).astype(jnp.bfloat16)
            left_c = jnp.dot(coupling, left_q, preferred_element_type=jnp.float32).astype(jnp.bfloat16)
            right_c = jnp.dot(coupling.T, right_q, preferred_element_type=jnp.float32).astype(jnp.bfloat16)
            pieces.append(jnp.dot(node_bases[2 * pair_idx], left_c, preferred_element_type=jnp.float32))
            pieces.append(jnp.dot(node_bases[2 * pair_idx + 1], right_c, preferred_element_type=jnp.float32))
        result = result + jnp.concatenate(pieces, axis=0)
    return result

def reference(signal, leaves, bases, couplings, weights):
    first = kernel_apply(signal, leaves, bases, couplings)
    scaled = (weights[:, None] * first).astype(jnp.bfloat16)
    return kernel_apply(scaled, leaves, bases, couplings).astype(jnp.bfloat16)
```

```python
import math

import jax
import jax.numpy as jnp
from jax import lax
from jax.experimental import pallas as pl
from jax.experimental.pallas import tpu as pltpu
from jax.sharding import PartitionSpec as P

LEAF = 512
NY = 4
CHIPS = 16
PLANES = 16
MESH = pl.DeviceIdType.MESH
GROUPS = ((0, 1), (1, 2), (2, 4))
F32 = jnp.float32
BF16 = jnp.bfloat16


def multi_wait(ref, sem):
    pltpu.make_async_copy(ref, ref, sem).wait()


def kernel(
    scales, x_hbm, leaves_hbm, bases_hbm, coup_hbm, w_hbm, out_ref,
    xv, bcat, lv, mraw, mor, wv, wcol, xs, acc, cb,
    p, rbuf, hs, rs, sv, zr, qt, ag, ag2,
    load_sem, send_sem, recv_sem,
):
    rows, width = xv.shape
    levels, rank = mor.shape[0], mor.shape[1]
    half = width // 2
    me = lax.axis_index("rows")
    core = me % 2
    chip = me // 2 % CHIPS
    cx, cy = chip // NY, chip % NY
    z = me // (2 * CHIPS)
    partner = me + 1 - 2 * core

    def plane_peer(d):
        q = (cx + d // NY) % NY * NY + (cy + d % NY) % NY
        return q, (z * CHIPS + q) * 2 + core

    def z_peer(level, i):
        s = (PLANES // 2) >> level
        mine = z // s
        other = mine + 1 - 2 * (mine % 2)
        zz = other * s + (z % s + i) % s
        return (zz * CHIPS + chip) * 2 + core

    loads = [pltpu.make_async_copy(x_hbm, xv, load_sem.at[0])]
    for l in range(levels):
        loads.append(pltpu.make_async_copy(
            bases_hbm.at[l], bcat.at[:, pl.ds(l * rank, rank)], load_sem.at[1 + l]))
    loads.append(pltpu.make_async_copy(leaves_hbm, lv, load_sem.at[5]))
    for l in range(levels):
        s = (PLANES // 2) >> l
        idx = (1 << l) - 1 + z // (2 * s)
        loads.append(pltpu.make_async_copy(coup_hbm.at[idx], mraw.at[l], load_sem.at[6 + l]))
    loads.append(pltpu.make_async_copy(w_hbm, wv, load_sem.at[10]))
    for c in loads:
        c.start()

    barrier = pltpu.get_barrier_semaphore()

    def tell(dev):
        pl.semaphore_signal(barrier, inc=1, device_id=(dev,), device_id_type=MESH)

    for l in range(levels):
        def tell_z(i, _):
            tell(z_peer(l, i))
            return 0
        lax.fori_loop(0, (PLANES // 2) >> l, tell_z, 0)

    def tell_plane(d, _):
        tell(plane_peer(d)[1])
        return 0
    lax.fori_loop(1, CHIPS, tell_plane, 0)
    tell(partner)

    def project(a, vec_ref):
        got = lax.dot_general(bcat[...], vec_ref[...], (((0,), (0,)), ((), ())),
                              preferred_element_type=F32)
        for h in range(2):
            for l in range(levels):
                p[a, h, l] = got[l * rank:(l + 1) * rank, h * half:(h + 1) * half]

    def remote(src, dst, a, phase, g, dev):
        pltpu.make_async_remote_copy(
            src_ref=src, dst_ref=dst, send_sem=send_sem.at[a, phase, g],
            recv_sem=recv_sem.at[a, phase, g], device_id=(dev,), device_id_type=MESH,
        ).start()

    def leaf_part(vec_ref):
        for b in range(rows // LEAF):
            sl = pl.ds(b * LEAF, LEAF)
            acc[sl, :] = jnp.dot(lv[sl, :], vec_ref[sl, :], preferred_element_type=F32)

    def coefficients(a, between):
        for g, (lo, hi) in enumerate(GROUPS):
            n = hi - lo
            remote(p.at[a, 1 - core, pl.ds(lo, n)], rbuf.at[a, pl.ds(lo, n)], a, 0, g, partner)
        for g, (lo, hi) in enumerate(GROUPS):
            n = hi - lo
            multi_wait(rbuf.at[a, pl.ds(lo, n)], recv_sem.at[a, 0, g])
            hs[a, lo:hi] = p[a, core, lo:hi] + rbuf[a, lo:hi]

            def send_rs(d, _):
                q, dev = plane_peer(d)
                remote(hs.at[a, pl.ds(lo, n), pl.ds(pl.multiple_of(q * 8, 8), 8)],
                       rs.at[a, d - 1, pl.ds(lo, n)], a, 1, g, dev)
                return 0
            lax.fori_loop(1, CHIPS, send_rs, 0)
        between()
        mine = pl.ds(pl.multiple_of(chip * 8, 8), 8)
        for g, (lo, hi) in enumerate(GROUPS):
            n = hi - lo
            multi_wait(rs.at[a, :, pl.ds(lo, n)], recv_sem.at[a, 1, g])
            total = hs[a, lo:hi, mine, :]
            for d in range(CHIPS - 1):
                total = total + rs[a, d, lo:hi]
            sv[a, lo:hi] = total
            for l in range(lo, hi):
                s = (PLANES // 2) >> l

                def send_z(i, _):
                    remote(sv.at[a, l], zr.at[a, s + i], a, 2, l, z_peer(l, i))
                    return 0
                lax.fori_loop(0, s, send_z, 0)
        for g, (lo, hi) in reversed(list(enumerate(GROUPS))):
            n = hi - lo
            for l in range(lo, hi):
                s = (PLANES // 2) >> l
                multi_wait(zr.at[a, pl.ds(s, s)], recv_sem.at[a, 2, l])
                total = zr[a, s]
                for i in range(1, s):
                    total = total + zr[a, s + i]
                total = total * scales[l]
                qt[a, l] = total
                ag[a, l, mine, :] = total

            def send_ag(d, _):
                q, dev = plane_peer(d)
                remote(qt.at[a, pl.ds(lo, n)], ag.at[a, pl.ds(lo, n), mine], a, 3, g, dev)
                return 0
            lax.fori_loop(1, CHIPS, send_ag, 0)
        for g, (lo, hi) in reversed(list(enumerate(GROUPS))):
            n = hi - lo
            multi_wait(ag.at[a, pl.ds(lo, n), pl.ds(0, 8 * (CHIPS - 1))], recv_sem.at[a, 3, g])
            remote(ag.at[a, pl.ds(lo, n)], ag2.at[a, pl.ds(lo, n)], a, 4, g, partner)
            for l in range(lo, hi):
                got = jnp.dot(mor[l], ag[a, l].astype(BF16), preferred_element_type=F32)
                cb[l * rank:(l + 1) * rank,
                   pl.ds(pl.multiple_of(core * half, half), half)] = got.astype(BF16)
        for g, (lo, hi) in reversed(list(enumerate(GROUPS))):
            n = hi - lo
            multi_wait(ag2.at[a, pl.ds(lo, n)], recv_sem.at[a, 4, g])
            for l in range(lo, hi):
                got = jnp.dot(mor[l], ag2[a, l].astype(BF16), preferred_element_type=F32)
                cb[l * rank:(l + 1) * rank,
                   pl.ds(pl.multiple_of((1 - core) * half, half), half)] = got.astype(BF16)

    for c in loads[:5]:
        c.wait()
    project(0, xv)
    pl.semaphore_wait(barrier, 2 * CHIPS - 1)

    def early():
        for c in loads[5:]:
            c.wait()
        leaf_part(xv)
        for l in range(levels):
            s = (PLANES // 2) >> l
            side = z // s % 2
            m = mraw[l].astype(F32)
            mor[l] = jnp.where(side == 0, m, m.T).astype(BF16)
        for r in range(rows // 128):
            row = jnp.broadcast_to(wv[r:r + 1, :], (128, 128))
            wcol[r * 128:(r + 1) * 128, :] = row.T

    coefficients(0, early)
    first = acc[...] + jnp.dot(bcat[...], cb[...], preferred_element_type=F32)
    for h in range(2):
        hl = slice(h * half, (h + 1) * half)
        xs[:, hl] = (wcol[...] * first[:, hl]).astype(BF16)
    project(1, xs)
    coefficients(1, lambda: leaf_part(xs))
    out_ref[...] = (acc[...] + jnp.dot(bcat[...], cb[...], preferred_element_type=F32)).astype(BF16)

    for a in range(2):
        for g, (lo, hi) in enumerate(GROUPS):
            n = hi - lo
            multi_wait(rbuf.at[a, pl.ds(lo, n)], send_sem.at[a, 0, g])
            multi_wait(rs.at[a, :, pl.ds(lo, n)], send_sem.at[a, 1, g])
            multi_wait(ag.at[a, pl.ds(lo, n), pl.ds(0, 8 * (CHIPS - 1))], send_sem.at[a, 3, g])
            multi_wait(ag2.at[a, pl.ds(lo, n)], send_sem.at[a, 4, g])
        for l in range(levels):
            s = (PLANES // 2) >> l
            multi_wait(zr.at[a, pl.ds(s, s)], send_sem.at[a, 2, l])


def on_device(signal, leaves, bases, couplings, weights):
    rows, width = signal.shape
    levels, _, rank = bases.shape
    count = lax.axis_size("rows")
    scales = [1.0 / math.sqrt(rows * (count >> level + 1) * rank) for level in range(levels)]
    half = width // 2
    vm = pltpu.VMEM
    anyspec = pl.BlockSpec(memory_space=pl.ANY)
    dma = pltpu.SemaphoreType.DMA

    def body(*refs):
        kernel(scales, *refs)

    return pl.pallas_call(
        body,
        name="double_product",
        out_shape=jax.ShapeDtypeStruct((rows, width), BF16),
        in_specs=[anyspec] * 5,
        out_specs=pl.BlockSpec(memory_space=vm),
        scratch_shapes=[
            vm((rows, width), BF16),
            vm((rows, levels * rank), BF16),
            vm((rows, LEAF), BF16),
            vm((levels, rank, rank), BF16),
            vm((levels, rank, rank), BF16),
            vm((rows // 128, 128), F32),
            vm((rows, 128), F32),
            vm((rows, width), BF16),
            vm((rows, width), F32),
            vm((levels * rank, width), BF16),
            vm((2, 2, levels, rank, half), F32),
            vm((2, levels, rank, half), F32),
            vm((2, levels, rank, half), F32),
            vm((2, CHIPS - 1, levels, 8, half), F32),
            vm((2, levels, 8, half), F32),
            vm((2, PLANES, 8, half), F32),
            vm((2, levels, 8, half), F32),
            vm((2, levels, rank, half), F32),
            vm((2, levels, rank, half), F32),
            dma((11,)),
            dma((2, 5, 4)),
            dma((2, 5, 4)),
        ],
        compiler_params=pltpu.CompilerParams(collective_id=0, has_side_effects=True),
    )(signal, leaves, bases, couplings, weights.reshape(rows // 128, 128))


def solution(mesh):
    in_specs = (P("rows", None), P("rows", None), P(None, "rows", None), P(), P("rows"))
    return jax.shard_map(
        on_device, mesh=mesh, in_specs=in_specs, out_specs=P("rows", None), check_vma=False
    )
```

```python
import math

import jax
import jax.numpy as jnp
from jax import lax
from jax.experimental import pallas as pl
from jax.experimental.pallas import tpu as pltpu
from jax.sharding import PartitionSpec as P

LEAF = 512
NY = 4
CHIPS = 16
PLANES = 16
MESH = pl.DeviceIdType.MESH
GROUPS = ((0, 1), (1, 2), (2, 4))
GRAM_FIRST = True
F32 = jnp.float32
BF16 = jnp.bfloat16


def multi_wait(ref, sem):
    pltpu.make_async_copy(ref, ref, sem).wait()
ORDER = tuple(reversed(tuple(enumerate(GROUPS))))
PAIR_P, RS_P, Z0, AG0, FWD0, PAIR_U, RS_U, PAIR_G, RS_G, PAIR_R, Z1, AG1, FWD1 = range(13)
TN = (((0,), (0,)), ((), ()))


def multi_wait(ref, sem):
    pltpu.make_async_copy(ref, ref, sem).wait()


def kernel(
    scales, x_hbm, leaves_hbm, bases_hbm, coup_hbm, w_hbm, out_ref,
    xv, bcat, lv, mraw, mor, wv, wcol, wb, ys, xs, acc, cb, ch,
    p, rbuf, hs, rs, u, ubuf, us, urs, g, gbuf, gs, grs, gm, gx, ghl, usum,
    sv, zr, qt, ag, ag2,
    load_sem, send_sem, recv_sem, round_sem,
):
    rows, width = xv.shape
    levels, rank = mor.shape[0], mor.shape[1]
    half = width // 2
    me = lax.axis_index("rows")
    core = me % 2
    chip = me // 2 % CHIPS
    cx, cy = chip // NY, chip % NY
    z = me // (2 * CHIPS)
    partner = me + 1 - 2 * core
    mine = pl.ds(pl.multiple_of(chip * 8, 8), 8)
    own_cols = pl.ds(pl.multiple_of(core * half, half), half)
    other_cols = pl.ds(pl.multiple_of((1 - core) * half, half), half)

    def plane_peer(d):
        q = (cx + d // NY) % NY * NY + (cy + d % NY) % NY
        return q, (z * CHIPS + q) * 2 + core

    def along_z(d):
        return ((z + d + PLANES) % PLANES * CHIPS + chip) * 2 + core

    def z_peer(level, i):
        s = (PLANES // 2) >> level
        side = z // s
        other = side + 1 - 2 * (side % 2)
        zz = other * s + (z % s + i) % s
        return (zz * CHIPS + chip) * 2 + core

    loads = [pltpu.make_async_copy(x_hbm, xv, load_sem.at[0])]
    for l in range(levels):
        loads.append(pltpu.make_async_copy(
            bases_hbm.at[l], bcat.at[:, pl.ds(l * rank, rank)], load_sem.at[1 + l]))
    loads.append(pltpu.make_async_copy(leaves_hbm, lv, load_sem.at[5]))
    for l in range(levels):
        s = (PLANES // 2) >> l
        idx = (1 << l) - 1 + z // (2 * s)
        loads.append(pltpu.make_async_copy(coup_hbm.at[idx], mraw.at[l], load_sem.at[6 + l]))
    loads.append(pltpu.make_async_copy(w_hbm, wv, load_sem.at[10]))
    for c in loads:
        c.start()

    barrier = pltpu.get_barrier_semaphore()

    def tell(dev):
        pl.semaphore_signal(barrier, inc=1, device_id=(dev,), device_id_type=MESH)

    def tell_plane(d, _):
        tell(plane_peer(d)[1])
        return 0
    lax.fori_loop(1, CHIPS, tell_plane, 0)
    tell(partner)
    for d in (1, -1):
        tell(along_z(d))

    def z_round(r):
        for d in (1 << r, -(1 << r)):
            pl.semaphore_signal(round_sem.at[r], inc=1, device_id=(along_z(d),), device_id_type=MESH)

    sent = []

    def remote(src, dst, phase, grp, dev):
        pltpu.make_async_remote_copy(
            src_ref=src, dst_ref=dst, send_sem=send_sem.at[phase, grp],
            recv_sem=recv_sem.at[phase, grp], device_id=(dev,), device_id_type=MESH,
        ).start()

    def arrived(ref, phase, grp):
        multi_wait(ref, recv_sem.at[phase, grp])
        sent.append((ref, phase, grp))

    def project(vec_ref, dst):
        got = lax.dot_general(bcat[...], vec_ref[...], TN, preferred_element_type=F32)
        for h in range(2):
            for l in range(levels):
                dst[h, l] = got[l * rank:(l + 1) * rank, h * half:(h + 1) * half]

    def leaf_part(vec_ref):
        for b in range(rows // LEAF):
            sl = pl.ds(b * LEAF, LEAF)
            acc[sl, :] = jnp.dot(lv[sl, :], vec_ref[sl, :], preferred_element_type=F32)

    def scatter(src, dst, phase, grp, lo, hi):
        def body(d, _):
            q, dev = plane_peer(d)
            remote(src.at[pl.ds(lo, hi - lo), pl.ds(pl.multiple_of(q * 8, 8), 8)],
                   dst.at[d - 1, pl.ds(lo, hi - lo)], phase, grp, dev)
            return 0
        lax.fori_loop(1, CHIPS, body, 0)

    def gathered_sum(src, buf, lo, hi):
        total = src[lo:hi, mine, :]
        for d in range(CHIPS - 1):
            total = total + buf[d, lo:hi]
        return total

    def z_send(a, l):
        s = (PLANES // 2) >> l

        def body(i, _):
            remote(sv.at[a, l], zr.at[a, s + i], (Z0, Z1)[a], l, z_peer(l, i))
            return 0
        lax.fori_loop(0, s, body, 0)

    def z_to_gather(a):
        for grp, (lo, hi) in ORDER:
            for l in range(lo, hi):
                s = (PLANES // 2) >> l
                arrived(zr.at[a, pl.ds(s, s)], (Z0, Z1)[a], l)
                total = zr[a, s]
                for i in range(1, s):
                    total = total + zr[a, s + i]
                total = total * scales[l]
                qt[a, l] = total
                ag[a, l, mine, :] = total

            def body(d, _):
                _, dev = plane_peer(d)
                remote(qt.at[a, pl.ds(lo, hi - lo)], ag.at[a, pl.ds(lo, hi - lo), mine],
                       (AG0, AG1)[a], grp, dev)
                return 0
            lax.fori_loop(1, CHIPS, body, 0)

    def couple(l, buf, cols):
        got = jnp.dot(mor[l], buf[l].astype(BF16), preferred_element_type=F32).astype(BF16)
        cb[l * rank:(l + 1) * rank, cols] = got
        return got

    def own_half(a):
        for grp, (lo, hi) in ORDER:
            arrived(ag.at[a, pl.ds(lo, hi - lo), pl.ds(0, 8 * (CHIPS - 1))], (AG0, AG1)[a], grp)
            remote(ag.at[a, pl.ds(lo, hi - lo)], ag2.at[a, pl.ds(lo, hi - lo)],
                   (FWD0, FWD1)[a], grp, partner)
            for l in range(lo, hi):
                ch[l * rank:(l + 1) * rank, :] = couple(l, ag.at[a], own_cols)

    def other_half(a):
        for grp, (lo, hi) in ORDER:
            arrived(ag2.at[a, pl.ds(lo, hi - lo)], (FWD0, FWD1)[a], grp)
            for l in range(lo, hi):
                couple(l, ag2.at[a], other_cols)

    for c in loads[:5]:
        c.wait()
    project(xv, p)
    pl.semaphore_wait(barrier, CHIPS + 2)
    for grp, (lo, hi) in enumerate(GROUPS):
        remote(p.at[1 - core, pl.ds(lo, hi - lo)], rbuf.at[pl.ds(lo, hi - lo)], PAIR_P, grp, partner)
    z_round(0)

    loads[10].wait()
    for r in range(rows // 128):
        row = jnp.broadcast_to(wv[r:r + 1, :], (128, 128))
        wcol[r * 128:(r + 1) * 128, :] = row.T
    for l in range(levels):
        cl = slice(l * rank, (l + 1) * rank)
        wb[:, cl] = (wcol[...] * bcat[:, cl].astype(F32)).astype(BF16)

    def gram():
        got = lax.dot_general(bcat[...], wb[...], TN, preferred_element_type=F32)
        for h in range(2):
            for l in range(levels):
                g[h, l] = got[l * rank:(l + 1) * rank, h * 2 * rank:(h + 1) * 2 * rank]
        remote(g.at[1 - core], gbuf, PAIR_G, 0, partner)

    if GRAM_FIRST:
        gram()
    for grp, (lo, hi) in enumerate(GROUPS):
        arrived(rbuf.at[pl.ds(lo, hi - lo)], PAIR_P, grp)
        hs[lo:hi] = p[core, lo:hi] + rbuf[lo:hi]
        scatter(hs, rs, RS_P, grp, lo, hi)
    if not GRAM_FIRST:
        gram()
    pl.semaphore_wait(round_sem.at[0], 2)
    z_round(1)

    loads[5].wait()
    leaf_part(xv)
    for h in range(2):
        hl = slice(h * half, (h + 1) * half)
        ys[:, hl] = (wcol[...] * acc[:, hl]).astype(BF16)
    project(ys, u)
    remote(u.at[1 - core], ubuf, PAIR_U, 0, partner)
    pl.semaphore_wait(round_sem.at[1], 2)
    z_round(2)
    arrived(gbuf, PAIR_G, 0)
    gs[...] = g[core] + gbuf[...]
    scatter(gs, grs, RS_G, 0, 0, levels)
    arrived(ubuf, PAIR_U, 0)
    us[...] = u[core] + ubuf[...]
    scatter(us, urs, RS_U, 0, 0, levels)

    pl.semaphore_wait(round_sem.at[2], 2)
    for grp, (lo, hi) in enumerate(GROUPS):
        arrived(rs.at[:, pl.ds(lo, hi - lo)], RS_P, grp)
        sv[0, lo:hi] = gathered_sum(hs, rs, lo, hi)
        for l in range(lo, hi):
            z_send(0, l)

    for c in loads[6:10]:
        c.wait()
    for l in range(levels):
        s = (PLANES // 2) >> l
        side = z // s % 2
        m = mraw[l].astype(F32)
        mor[l] = jnp.where(side == 0, m, m.T).astype(BF16)

    z_to_gather(0)
    arrived(grs, RS_G, 0)
    gm[...] = gathered_sum(gs, grs, 0, levels)
    remote(gm, gx, PAIR_R, 0, partner)
    arrived(urs, RS_U, 0)
    usum[...] = gathered_sum(us, urs, 0, levels)
    arrived(gx, PAIR_R, 0)
    for k in range(2):
        full = jnp.where(core == k, gm[...], gx[...]).reshape(levels * 8, 2 * rank)
        hi_part = full.astype(BF16)
        ghl[0, k] = hi_part
        ghl[1, k] = (full - hi_part.astype(F32)).astype(BF16)

    own_half(0)
    nxt = usum[...].reshape(levels * 8, half)
    for k in range(2):
        cols = ch[k * 2 * rank:(k + 1) * 2 * rank, :]
        for part in range(2):
            nxt = nxt + jnp.dot(ghl[part, k], cols, preferred_element_type=F32)
    sv[1] = nxt.reshape(levels, 8, half)
    for l in range(levels):
        z_send(1, l)

    other_half(0)
    first = acc[...] + jnp.dot(bcat[...], cb[...], preferred_element_type=F32)
    for h in range(2):
        hl = slice(h * half, (h + 1) * half)
        xs[:, hl] = (wcol[...] * first[:, hl]).astype(BF16)
    leaf_part(xs)

    z_to_gather(1)
    own_half(1)
    other_half(1)
    out_ref[...] = (acc[...] + jnp.dot(bcat[...], cb[...], preferred_element_type=F32)).astype(BF16)
    for ref, phase, grp in sent:
        multi_wait(ref, send_sem.at[phase, grp])


def on_device(signal, leaves, bases, couplings, weights):
    rows, width = signal.shape
    levels, _, rank = bases.shape
    count = lax.axis_size("rows")
    scales = [1.0 / math.sqrt(rows * (count >> level + 1) * rank) for level in range(levels)]
    half = width // 2
    vm = pltpu.VMEM
    anyspec = pl.BlockSpec(memory_space=pl.ANY)
    dma = pltpu.SemaphoreType.DMA

    def body(*refs):
        kernel(scales, *refs)

    return pl.pallas_call(
        body,
        name="double_product",
        out_shape=vm((rows, width), BF16),
        in_specs=[anyspec] * 5,
        out_specs=pl.BlockSpec(memory_space=vm),
        scratch_shapes=[
            vm((rows, width), BF16),
            vm((rows, levels * rank), BF16),
            vm((rows, LEAF), BF16),
            vm((levels, rank, rank), BF16),
            vm((levels, rank, rank), BF16),
            vm((rows // 128, 128), F32),
            vm((rows, 128), F32),
            vm((rows, levels * rank), BF16),
            vm((rows, width), BF16),
            vm((rows, width), BF16),
            vm((rows, width), F32),
            vm((levels * rank, width), BF16),
            vm((levels * rank, half), BF16),
            vm((2, levels, rank, half), F32),
            vm((levels, rank, half), F32),
            vm((levels, rank, half), F32),
            vm((CHIPS - 1, levels, 8, half), F32),
            vm((2, levels, rank, half), F32),
            vm((levels, rank, half), F32),
            vm((levels, rank, half), F32),
            vm((CHIPS - 1, levels, 8, half), F32),
            vm((2, levels, rank, 2 * rank), F32),
            vm((levels, rank, 2 * rank), F32),
            vm((levels, rank, 2 * rank), F32),
            vm((CHIPS - 1, levels, 8, 2 * rank), F32),
            vm((levels, 8, 2 * rank), F32),
            vm((levels, 8, 2 * rank), F32),
            vm((2, 2, levels * 8, 2 * rank), BF16),
            vm((levels, 8, half), F32),
            vm((2, levels, 8, half), F32),
            vm((2, PLANES, 8, half), F32),
            vm((2, levels, 8, half), F32),
            vm((2, levels, rank, half), F32),
            vm((2, levels, rank, half), F32),
            dma((11,)),
            dma((13, 4)),
            dma((13, 4)),
            pltpu.SemaphoreType.REGULAR((3,)),
        ],
        compiler_params=pltpu.CompilerParams(collective_id=0, has_side_effects=True),
    )(signal, leaves, bases, couplings, weights.reshape(rows // 128, 128))


def solution(mesh):
    in_specs = (P("rows", None), P("rows", None), P(None, "rows", None), P(), P("rows"))
    return jax.shard_map(
        on_device, mesh=mesh, in_specs=in_specs, out_specs=P("rows", None), check_vma=False
    )
```

```python
import math

import jax
import jax.numpy as jnp
from jax import lax
from jax.experimental import pallas as pl
from jax.experimental.pallas import tpu as pltpu
from jax.sharding import PartitionSpec as P

LEAF = 512
NY = 4
CHIPS = 16
PLANES = 16
MESH = pl.DeviceIdType.MESH
GROUPS = ((0, 1), (1, 2), (2, 4))
F32 = jnp.float32
BF16 = jnp.bfloat16


ORDER = tuple(reversed(tuple(enumerate(GROUPS))))
OFFSETS = sorted(
    ((dx, dy) for dx in range(NY) for dy in range(NY) if dx or dy),
    key=lambda o: -min(o[0], NY - o[0]) - min(o[1], NY - o[1]),
)
PAIR_P, RS_P, Z0, AG0, FWD0, PAIR_U, RS_U, PAIR_G, RS_G, PAIR_R, Z1, AG1, FWD1 = range(13)
TN = (((0,), (0,)), ((), ()))


def multi_wait(ref, sem):
    pltpu.make_async_copy(ref, ref, sem).wait()


def kernel(
    scales, x_hbm, leaves_hbm, bases_hbm, coup_hbm, w_hbm, out_ref,
    xv, bcat, lv, mraw, mor, wv, wcol, wb, ys, xs, acc, cb,
    p, rbuf, hs, rs, rs0, u, ubuf, us, urs, g, gbuf, gs, grs, gm, gx, ghl, usum,
    sv, zr, qt, ag, ag2,
    load_sem, send_sem, recv_sem, pair_sem,
):
    rows, width = xv.shape
    levels, rank = mor.shape[0], mor.shape[1]
    half = width // 2
    me = lax.axis_index("rows")
    core = me % 2
    chip = me // 2 % CHIPS
    cx, cy = chip // NY, chip % NY
    z = me // (2 * CHIPS)
    partner = me + 1 - 2 * core
    mine = pl.ds(pl.multiple_of(chip * 8, 8), 8)
    own_cols = pl.ds(pl.multiple_of(core * half, half), half)
    other_cols = pl.ds(pl.multiple_of((1 - core) * half, half), half)

    xq = [(cx + d) % NY * NY for d in range(NY)]
    yq = [(cy + d) % NY for d in range(NY)]
    plane0 = z * (2 * CHIPS) + core
    peers = []
    for dx, dy in OFFSETS:
        q = xq[dx] + yq[dy]
        peers.append((pl.multiple_of(q * 8, 8), plane0 + q * 2))
    column0 = chip * 2 + core
    siblings = []
    for l in range(levels):
        s = (PLANES // 2) >> l
        side = z // s
        right = side % 2
        other = (side + 1 - 2 * right) * s
        devs = []
        for t in range(s):
            if l == 0:
                i = (t + 1) // 2 if t % 2 else s - t // 2
                at = (z + i) % s
            else:
                at = right * t + (1 - right) * (s - 1 - t)
            devs.append((other + at) * (2 * CHIPS) + column0)
        siblings.append((s, z % s, devs))

    hrows = rows // 2
    first_loads = []
    for r in range(2):
        rl = pl.ds(r * hrows, hrows)
        part = [pltpu.make_async_copy(x_hbm.at[rl], xv.at[rl], load_sem.at[5 * r])]
        for l in range(levels):
            part.append(pltpu.make_async_copy(
                bases_hbm.at[l, rl], bcat.at[rl, pl.ds(l * rank, rank)], load_sem.at[5 * r + 1 + l]))
        first_loads.append(part)
    w_load = pltpu.make_async_copy(w_hbm, wv, load_sem.at[10])
    leaf_load = pltpu.make_async_copy(leaves_hbm, lv, load_sem.at[11])
    m_loads = []
    for l in range(levels):
        s = (PLANES // 2) >> l
        idx = (1 << l) - 1 + z // (2 * s)
        m_loads.append(pltpu.make_async_copy(coup_hbm.at[idx], mraw.at[l], load_sem.at[12 + l]))
    for part in first_loads:
        for c in part:
            c.start()
    w_load.start()

    barrier = pltpu.get_barrier_semaphore()

    def tell(dev):
        pl.semaphore_signal(barrier, inc=1, device_id=(dev,), device_id_type=MESH)

    def tell(dev):
        pl.semaphore_signal(barrier, inc=1, device_id=(dev,), device_id_type=MESH)

    for _, _, devs in siblings:
        for dev in devs:
            tell(dev - core + 1)
    for _, dev in peers:
        tell(dev - core)
    tell(partner)

    def heard():
        pl.semaphore_wait(barrier, 2 * CHIPS - 1)
        pl.semaphore_signal(pair_sem, inc=1, device_id=(partner,), device_id_type=MESH)

    def know(heard_by):
        @pl.when(core == heard_by)
        def _():
            heard()

        @pl.when(core != heard_by)
        def _():
            pl.semaphore_wait(pair_sem, 1)

    sent = []

    def remote(src, dst, phase, grp, dev):
        pltpu.make_async_remote_copy(
            src_ref=src, dst_ref=dst, send_sem=send_sem.at[phase, grp],
            recv_sem=recv_sem.at[phase, grp], device_id=(dev,), device_id_type=MESH,
        ).start()

    def arrived(ref, phase, grp):
        multi_wait(ref, recv_sem.at[phase, grp])
        sent.append((ref, phase, grp))

    def project(vec_ref, dst):
        got = lax.dot_general(bcat[...], vec_ref[...], TN, preferred_element_type=F32)
        for h in range(2):
            for l in range(levels):
                dst[h, l] = got[l * rank:(l + 1) * rank, h * half:(h + 1) * half]

    def leaf_part(vec_ref):
        for b in range(rows // LEAF):
            sl = pl.ds(b * LEAF, LEAF)
            acc[sl, :] = jnp.dot(lv[sl, :], vec_ref[sl, :], preferred_element_type=F32)

    def scatter(src, dst, phase, grp, lo, hi):
        for d, (row, dev) in enumerate(peers):
            remote(src.at[pl.ds(lo, hi - lo), pl.ds(row, 8)], dst.at[d, pl.ds(lo, hi - lo)],
                   phase, grp, dev)

    def gathered_sum(src, buf, lo, hi):
        total = src[lo:hi, mine, :]
        for d in range(CHIPS - 1):
            total = total + buf[d, lo:hi]
        return total

    def z_send(a, l):
        s, place, devs = siblings[l]
        for dev in devs:
            remote(sv.at[a, l], zr.at[a, s + place], (Z0, Z1)[a], l, dev)

    def both_cores(a, grp):
        return a == 1 and grp == ORDER[-1][0]

    def z_to_gather(a):
        for grp, (lo, hi) in ORDER:
            for l in range(lo, hi):
                s = (PLANES // 2) >> l
                arrived(zr.at[a, pl.ds(s, s)], (Z0, Z1)[a], l)
                total = zr[a, s]
                for i in range(1, s):
                    total = total + zr[a, s + i]
                total = total * scales[l]
                qt[a, l] = total
                ag[a, l, mine, :] = total

            for _, dev in peers:
                remote(qt.at[a, pl.ds(lo, hi - lo)], ag.at[a, pl.ds(lo, hi - lo), mine],
                       (AG0, AG1)[a], grp, dev)
            if both_cores(a, grp):
                for _, dev in peers:
                    remote(qt.at[a, pl.ds(lo, hi - lo)], ag2.at[a, pl.ds(lo, hi - lo), mine],
                           (FWD0, FWD1)[a], grp, dev + 1 - 2 * core)
            if both_cores(a, grp):
                remote(qt.at[a, pl.ds(lo, hi - lo)], ag2.at[a, pl.ds(lo, hi - lo), mine],
                       (FWD0, FWD1)[a], grp, partner)

    def couple(l, buf, cols):
        got = jnp.dot(mor[l], buf[l].astype(BF16), preferred_element_type=F32).astype(BF16)
        cb[l * rank:(l + 1) * rank, cols] = got
        return got

    def own_group(a, grp, lo, hi):
        arrived(ag.at[a, pl.ds(lo, hi - lo), pl.ds(0, 8 * (CHIPS - 1))], (AG0, AG1)[a], grp)
        if not both_cores(a, grp):
            remote(ag.at[a, pl.ds(lo, hi - lo)], ag2.at[a, pl.ds(lo, hi - lo)],
                   (FWD0, FWD1)[a], grp, partner)
        return [(l, couple(l, ag.at[a], own_cols)) for l in range(lo, hi)]

    def other_group(a, grp, lo, hi):
        arrived(ag2.at[a, pl.ds(lo, hi - lo)], (FWD0, FWD1)[a], grp)
        for l in range(lo, hi):
            couple(l, ag2.at[a], other_cols)

    def expand(lo, hi):
        kl = slice(lo * rank, hi * rank)
        return jnp.dot(bcat[:, kl], cb[kl, :], preferred_element_type=F32)

    got = None
    for r in range(2):
        for c in first_loads[r]:
            c.wait()
        rl = slice(r * hrows, (r + 1) * hrows)
        more = lax.dot_general(bcat[rl, :], xv[rl, :], TN, preferred_element_type=F32)
        got = more if got is None else got + more
    for h in range(2):
        for l in range(levels):
            p[h, l] = got[l * rank:(l + 1) * rank, h * half:(h + 1) * half]
    know(0)
    for grp, (lo, hi) in enumerate(GROUPS):
        if grp == 0:
            for d, (row, dev) in enumerate(peers):
                remote(p.at[core, 0, pl.ds(row, 8)], rs0.at[d], RS_P, grp, dev)
                remote(p.at[1 - core, 0, pl.ds(row, 8)], rs0.at[CHIPS - 1 + d], RS_P, grp,
                       dev + 1 - 2 * core)
            remote(p.at[1 - core, 0, mine], rs0.at[2 * CHIPS - 2], RS_P, grp, partner)
            continue
        remote(p.at[1 - core, pl.ds(lo, hi - lo)], rbuf.at[pl.ds(lo, hi - lo)], PAIR_P, grp, partner)
    leaf_load.start()
    for c in m_loads:
        c.start()

    w_load.wait()
    for r in range(rows // 128):
        row = jnp.broadcast_to(wv[r:r + 1, :], (128, 128))
        wcol[r * 128:(r + 1) * 128, :] = row.T
    for l in range(levels):
        cl = slice(l * rank, (l + 1) * rank)
        wb[:, cl] = (wcol[...] * bcat[:, cl].astype(F32)).astype(BF16)

    def gram():
        got = lax.dot_general(bcat[...], wb[...], TN, preferred_element_type=F32)
        for h in range(2):
            for l in range(levels):
                g[h, l] = got[l * rank:(l + 1) * rank, h * 2 * rank:(h + 1) * 2 * rank]
        remote(g.at[1 - core], gbuf, PAIR_G, 0, partner)

    gram()
    for grp, (lo, hi) in enumerate(GROUPS):
        if grp == 0:
            continue
        arrived(rbuf.at[pl.ds(lo, hi - lo)], PAIR_P, grp)
        hs[lo:hi] = p[core, lo:hi] + rbuf[lo:hi]
        scatter(hs, rs, RS_P, grp, lo, hi)

    leaf_load.wait()
    leaf_part(xv)
    for h in range(2):
        hl = slice(h * half, (h + 1) * half)
        ys[:, hl] = (wcol[...] * acc[:, hl]).astype(BF16)
    project(ys, u)
    remote(u.at[1 - core], ubuf, PAIR_U, 0, partner)
    arrived(gbuf, PAIR_G, 0)
    gs[...] = g[core] + gbuf[...]
    scatter(gs, grs, RS_G, 0, 0, levels)

    know(1)
    for grp, (lo, hi) in enumerate(GROUPS):
        if grp == 0:
            arrived(rs0, RS_P, grp)
            total = p[core, 0, mine, :]
            for d in range(2 * CHIPS - 1):
                total = total + rs0[d]
            sv[0, 0] = total
        else:
            arrived(rs.at[:, pl.ds(lo, hi - lo)], RS_P, grp)
            sv[0, lo:hi] = gathered_sum(hs, rs, lo, hi)
        for l in range(lo, hi):
            z_send(0, l)

    arrived(ubuf, PAIR_U, 0)
    us[...] = u[core] + ubuf[...]
    scatter(us, urs, RS_U, 0, 0, levels)
    for c in m_loads:
        c.wait()
    for l in range(levels):
        s = (PLANES // 2) >> l
        side = z // s % 2
        m = mraw[l].astype(F32)
        mor[l] = jnp.where(side == 0, m, m.T).astype(BF16)

    z_to_gather(0)
    arrived(grs, RS_G, 0)
    gm[...] = gathered_sum(gs, grs, 0, levels)
    remote(gm, gx, PAIR_R, 0, partner)
    arrived(urs, RS_U, 0)
    usum[...] = gathered_sum(us, urs, 0, levels)
    arrived(gx, PAIR_R, 0)
    for k in range(2):
        full = jnp.where(core == k, gm[...], gx[...]).reshape(levels * 8, 2 * rank)
        hi_part = full.astype(BF16)
        low_part = (full - hi_part.astype(F32)).astype(BF16)
        for j in range(2):
            jl = slice(j * rank, (j + 1) * rank)
            ghl[2 * k + j, :levels * 8] = hi_part[:, jl]
            ghl[2 * k + j, levels * 8:] = low_part[:, jl]

    nxt = usum[...].reshape(levels * 8, half)
    for grp, (lo, hi) in ORDER:
        for l, cols in own_group(0, grp, lo, hi):
            both = jnp.dot(ghl[l], cols, preferred_element_type=F32)
            nxt = nxt + (both[:levels * 8] + both[levels * 8:])
    sv[1] = nxt.reshape(levels, 8, half)
    for l in range(levels):
        z_send(1, l)

    for grp, (lo, hi) in ORDER:
        other_group(0, grp, lo, hi)
    first = acc[...] + expand(0, levels)
    for h in range(2):
        hl = slice(h * half, (h + 1) * half)
        xs[:, hl] = (wcol[...] * first[:, hl]).astype(BF16)
    leaf_part(xs)

    z_to_gather(1)
    last = len(ORDER) - 1
    for n, (grp, (lo, hi)) in enumerate(ORDER):
        own_group(1, grp, lo, hi)
        if n >= 1:
            pgrp, (plo, phi) = ORDER[n - 1]
            other_group(1, pgrp, plo, phi)
            acc[...] += expand(plo, phi)
    grp, (lo, hi) = ORDER[last]
    other_group(1, grp, lo, hi)
    out_ref[...] = (acc[...] + expand(lo, hi)).astype(BF16)
    for ref, phase, grp in sent:
        multi_wait(ref, send_sem.at[phase, grp])


def on_device(signal, leaves, bases, couplings, weights):
    rows, width = signal.shape
    levels, _, rank = bases.shape
    count = lax.axis_size("rows")
    scales = [1.0 / math.sqrt(rows * (count >> level + 1) * rank) for level in range(levels)]
    half = width // 2
    vm = pltpu.VMEM
    anyspec = pl.BlockSpec(memory_space=pl.ANY)
    dma = pltpu.SemaphoreType.DMA

    def body(*refs):
        kernel(scales, *refs)

    return pl.pallas_call(
        body,
        name="double_product",
        out_shape=vm((rows, width), BF16),
        in_specs=[anyspec] * 5,
        out_specs=pl.BlockSpec(memory_space=vm),
        scratch_shapes=[
            vm((rows, width), BF16),
            vm((rows, levels * rank), BF16),
            vm((rows, LEAF), BF16),
            vm((levels, rank, rank), BF16),
            vm((levels, rank, rank), BF16),
            vm((rows // 128, 128), F32),
            vm((rows, 128), F32),
            vm((rows, levels * rank), BF16),
            vm((rows, width), BF16),
            vm((rows, width), BF16),
            vm((rows, width), F32),
            vm((levels * rank, width), BF16),
            vm((2, levels, rank, half), F32),
            vm((levels, rank, half), F32),
            vm((levels, rank, half), F32),
            vm((CHIPS - 1, levels, 8, half), F32),
            vm((2 * CHIPS - 1, 8, half), F32),
            vm((2, levels, rank, half), F32),
            vm((levels, rank, half), F32),
            vm((levels, rank, half), F32),
            vm((CHIPS - 1, levels, 8, half), F32),
            vm((2, levels, rank, 2 * rank), F32),
            vm((levels, rank, 2 * rank), F32),
            vm((levels, rank, 2 * rank), F32),
            vm((CHIPS - 1, levels, 8, 2 * rank), F32),
            vm((levels, 8, 2 * rank), F32),
            vm((levels, 8, 2 * rank), F32),
            vm((levels, 2 * levels * 8, rank), BF16),
            vm((levels, 8, half), F32),
            vm((2, levels, 8, half), F32),
            vm((2, PLANES, 8, half), F32),
            vm((2, levels, 8, half), F32),
            vm((2, levels, rank, half), F32),
            vm((2, levels, rank, half), F32),
            dma((16,)),
            dma((13, 4)),
            dma((13, 4)),
            pltpu.SemaphoreType.REGULAR,
        ],
        compiler_params=pltpu.CompilerParams(collective_id=0, has_side_effects=True),
    )(signal, leaves, bases, couplings, weights.reshape(rows // 128, 128))


def solution(mesh):
    in_specs = (P("rows", None), P("rows", None), P(None, "rows", None), P(), P("rows"))
    return jax.shard_map(
        on_device, mesh=mesh, in_specs=in_specs, out_specs=P("rows", None), check_vma=False
    )
```

```python
import math

import jax
import jax.numpy as jnp
from jax import lax
from jax.experimental import pallas as pl
from jax.experimental.pallas import tpu as pltpu
from jax.sharding import PartitionSpec as P

LEAF = 512
NY = 4
CHIPS = 16
PLANES = 16
MESH = pl.DeviceIdType.MESH
GROUPS = ((0, 1), (1, 2), (2, 4))
F32 = jnp.float32
BF16 = jnp.bfloat16


ORDER = tuple(reversed(tuple(enumerate(GROUPS))))
OFFSETS = sorted(
    ((dx, dy) for dx in range(NY) for dy in range(NY) if dx or dy),
    key=lambda o: -min(o[0], NY - o[0]) - min(o[1], NY - o[1]),
)
PAIR_P, RS_P, Z0, AG0, FWD0, PAIR_U, RS_U, PAIR_G, RS_G, PAIR_R, Z1, AG1, FWD1 = range(13)
TN = (((0,), (0,)), ((), ()))


def multi_wait(ref, sem):
    pltpu.make_async_copy(ref, ref, sem).wait()


def kernel(
    scales, x_hbm, leaves_hbm, bases_hbm, coup_hbm, w_hbm, out_ref,
    xv, bcat, lv, mraw, mor, wv, wcol, wb, ys, xs, acc, cb,
    p, rbuf, hs, rs, rs0, u, ubuf, us, urs, g, gbuf, gs, grs, gm, gx, ghl, usum,
    sv, zr, qt, ag, ag2,
    load_sem, send_sem, recv_sem, pair_sem,
):
    rows, width = xv.shape
    levels, rank = mor.shape[0], mor.shape[1]
    half = width // 2
    me = lax.axis_index("rows")
    core = me % 2
    chip = me // 2 % CHIPS
    cx, cy = chip // NY, chip % NY
    z = me // (2 * CHIPS)
    partner = me + 1 - 2 * core
    mine = pl.ds(pl.multiple_of(chip * 8, 8), 8)
    own_cols = pl.ds(pl.multiple_of(core * half, half), half)
    other_cols = pl.ds(pl.multiple_of((1 - core) * half, half), half)

    xq = [(cx + d) % NY * NY for d in range(NY)]
    yq = [(cy + d) % NY for d in range(NY)]
    plane0 = z * (2 * CHIPS) + core
    peers = []
    for dx, dy in OFFSETS:
        q = xq[dx] + yq[dy]
        peers.append((pl.multiple_of(q * 8, 8), plane0 + q * 2))
    column0 = chip * 2 + core
    siblings = []
    for l in range(levels):
        s = (PLANES // 2) >> l
        side = z // s
        right = side % 2
        other = (side + 1 - 2 * right) * s
        devs = []
        for t in range(s):
            if l == 0:
                i = (t + 1) // 2 if t % 2 else s - t // 2
                at = (z + i) % s
            else:
                at = right * t + (1 - right) * (s - 1 - t)
            devs.append((other + at) * (2 * CHIPS) + column0)
        siblings.append((s, z % s, devs))

    hrows = rows // 2
    first_loads = []
    for r in range(2):
        rl = pl.ds(r * hrows, hrows)
        part = [pltpu.make_async_copy(x_hbm.at[rl], xv.at[rl], load_sem.at[5 * r])]
        for l in range(levels):
            part.append(pltpu.make_async_copy(
                bases_hbm.at[l, rl], bcat.at[rl, pl.ds(l * rank, rank)], load_sem.at[5 * r + 1 + l]))
        first_loads.append(part)
    w_load = pltpu.make_async_copy(w_hbm, wv, load_sem.at[10])
    leaf_load = pltpu.make_async_copy(leaves_hbm, lv, load_sem.at[11])
    m_loads = []
    for l in range(levels):
        s = (PLANES // 2) >> l
        idx = (1 << l) - 1 + z // (2 * s)
        m_loads.append(pltpu.make_async_copy(coup_hbm.at[idx], mraw.at[l], load_sem.at[12 + l]))
    for part in first_loads:
        for c in part:
            c.start()
    w_load.start()

    barrier = pltpu.get_barrier_semaphore()

    def tell(dev):
        pl.semaphore_signal(barrier, inc=1, device_id=(dev,), device_id_type=MESH)

    def tell(dev):
        pl.semaphore_signal(barrier, inc=1, device_id=(dev,), device_id_type=MESH)

    for _, _, devs in siblings:
        for dev in devs:
            tell(dev - core + 1)
    for _, dev in peers:
        tell(dev - core)
    tell(partner)

    def heard():
        pl.semaphore_wait(barrier, 2 * CHIPS - 1)
        pl.semaphore_signal(pair_sem, inc=1, device_id=(partner,), device_id_type=MESH)

    def know(heard_by):
        @pl.when(core == heard_by)
        def _():
            heard()

        @pl.when(core != heard_by)
        def _():
            pl.semaphore_wait(pair_sem, 1)

    sent = []

    def remote(src, dst, phase, grp, dev):
        pltpu.make_async_remote_copy(
            src_ref=src, dst_ref=dst, send_sem=send_sem.at[phase, grp],
            recv_sem=recv_sem.at[phase, grp], device_id=(dev,), device_id_type=MESH,
        ).start()

    def arrived(ref, phase, grp):
        multi_wait(ref, recv_sem.at[phase, grp])
        sent.append((ref, phase, grp))

    def project(vec_ref, dst):
        got = lax.dot_general(bcat[...], vec_ref[...], TN, preferred_element_type=F32)
        for h in range(2):
            for l in range(levels):
                dst[h, l] = got[l * rank:(l + 1) * rank, h * half:(h + 1) * half]

    def leaf_part(vec_ref):
        for b in range(rows // LEAF):
            sl = pl.ds(b * LEAF, LEAF)
            acc[sl, :] = jnp.dot(lv[sl, :], vec_ref[sl, :], preferred_element_type=F32)

    def scatter(src, dst, phase, grp, lo, hi):
        for d, (row, dev) in enumerate(peers):
            remote(src.at[pl.ds(lo, hi - lo), pl.ds(row, 8)], dst.at[d, pl.ds(lo, hi - lo)],
                   phase, grp, dev)

    def gathered_sum(src, buf, lo, hi):
        total = src[lo:hi, mine, :]
        for d in range(CHIPS - 1):
            total = total + buf[d, lo:hi]
        return total

    def z_send(a, l):
        s, place, devs = siblings[l]
        for dev in devs:
            remote(sv.at[a, l], zr.at[a, s + place], (Z0, Z1)[a], l, dev)

    def both_cores(a, grp):
        return a == 1 and grp == ORDER[-1][0]

    def z_to_gather(a):
        for grp, (lo, hi) in ORDER:
            for l in range(lo, hi):
                s = (PLANES // 2) >> l
                arrived(zr.at[a, pl.ds(s, s)], (Z0, Z1)[a], l)
                total = zr[a, s]
                for i in range(1, s):
                    total = total + zr[a, s + i]
                total = total * scales[l]
                qt[a, l] = total
                ag[a, l, mine, :] = total

            for _, dev in peers:
                remote(qt.at[a, pl.ds(lo, hi - lo)], ag.at[a, pl.ds(lo, hi - lo), mine],
                       (AG0, AG1)[a], grp, dev)
            if both_cores(a, grp):
                for _, dev in peers:
                    remote(qt.at[a, pl.ds(lo, hi - lo)], ag2.at[a, pl.ds(lo, hi - lo), mine],
                           (FWD0, FWD1)[a], grp, dev + 1 - 2 * core)
            if both_cores(a, grp):
                remote(qt.at[a, pl.ds(lo, hi - lo)], ag2.at[a, pl.ds(lo, hi - lo), mine],
                       (FWD0, FWD1)[a], grp, partner)

    def couple(l, buf, cols):
        got = jnp.dot(mor[l], buf[l].astype(BF16), preferred_element_type=F32).astype(BF16)
        cb[l * rank:(l + 1) * rank, cols] = got
        return got

    def own_group(a, grp, lo, hi):
        arrived(ag.at[a, pl.ds(lo, hi - lo), pl.ds(0, 8 * (CHIPS - 1))], (AG0, AG1)[a], grp)
        if not both_cores(a, grp):
            remote(ag.at[a, pl.ds(lo, hi - lo)], ag2.at[a, pl.ds(lo, hi - lo)],
                   (FWD0, FWD1)[a], grp, partner)
        return [(l, couple(l, ag.at[a], own_cols)) for l in range(lo, hi)]

    def other_group(a, grp, lo, hi):
        arrived(ag2.at[a, pl.ds(lo, hi - lo)], (FWD0, FWD1)[a], grp)
        for l in range(lo, hi):
            couple(l, ag2.at[a], other_cols)

    def expand(lo, hi):
        kl = slice(lo * rank, hi * rank)
        return jnp.dot(bcat[:, kl], cb[kl, :], preferred_element_type=F32)

    got = None
    for r in range(2):
        for c in first_loads[r]:
            c.wait()
        rl = slice(r * hrows, (r + 1) * hrows)
        more = lax.dot_general(bcat[rl, :], xv[rl, :], TN, preferred_element_type=F32)
        got = more if got is None else got + more
    for h in range(2):
        for l in range(levels):
            p[h, l] = got[l * rank:(l + 1) * rank, h * half:(h + 1) * half]
    know(0)
    for grp, (lo, hi) in enumerate(GROUPS):
        if grp == 0:
            for d, (row, dev) in enumerate(peers):
                remote(p.at[core, 0, pl.ds(row, 8)], rs0.at[d], RS_P, grp, dev)
                remote(p.at[1 - core, 0, pl.ds(row, 8)], rs0.at[CHIPS - 1 + d], RS_P, grp,
                       dev + 1 - 2 * core)
            remote(p.at[1 - core, 0, mine], rs0.at[2 * CHIPS - 2], RS_P, grp, partner)
            continue
        remote(p.at[1 - core, pl.ds(lo, hi - lo)], rbuf.at[pl.ds(lo, hi - lo)], PAIR_P, grp, partner)
    leaf_load.start()
    for c in m_loads:
        c.start()

    w_load.wait()
    for r in range(rows // 128):
        row = jnp.broadcast_to(wv[r:r + 1, :], (128, 128))
        wcol[r * 128:(r + 1) * 128, :] = row.T
    for l in range(levels):
        cl = slice(l * rank, (l + 1) * rank)
        wb[:, cl] = (wcol[...] * bcat[:, cl].astype(F32)).astype(BF16)

    def gram():
        got = lax.dot_general(bcat[...], wb[...], TN, preferred_element_type=F32)
        for h in range(2):
            for l in range(levels):
                g[h, l] = got[l * rank:(l + 1) * rank, h * 2 * rank:(h + 1) * 2 * rank]

    gram()
    for l in range(levels):
        remote(g.at[1 - core, l], gbuf.at[l], PAIR_G, l, partner)
    for grp, (lo, hi) in enumerate(GROUPS):
        if grp == 0:
            continue
        arrived(rbuf.at[pl.ds(lo, hi - lo)], PAIR_P, grp)
        hs[lo:hi] = p[core, lo:hi] + rbuf[lo:hi]
        scatter(hs, rs, RS_P, grp, lo, hi)

    for l in range(levels):
        arrived(gbuf.at[l], PAIR_G, l)
        gs[l] = g[core, l] + gbuf[l]
        scatter(gs, grs, RS_G, l, l, l + 1)
    leaf_load.wait()
    leaf_part(xv)
    for h in range(2):
        hl = slice(h * half, (h + 1) * half)
        ys[:, hl] = (wcol[...] * acc[:, hl]).astype(BF16)
    project(ys, u)
    remote(u.at[1 - core], ubuf, PAIR_U, 0, partner)

    know(1)
    for grp, (lo, hi) in enumerate(GROUPS):
        if grp == 0:
            arrived(rs0, RS_P, grp)
            total = p[core, 0, mine, :]
            for d in range(2 * CHIPS - 1):
                total = total + rs0[d]
            sv[0, 0] = total
        else:
            arrived(rs.at[:, pl.ds(lo, hi - lo)], RS_P, grp)
            sv[0, lo:hi] = gathered_sum(hs, rs, lo, hi)
        for l in range(lo, hi):
            z_send(0, l)

    arrived(ubuf, PAIR_U, 0)
    us[...] = u[core] + ubuf[...]
    scatter(us, urs, RS_U, 0, 0, levels)
    for c in m_loads:
        c.wait()
    for l in range(levels):
        s = (PLANES // 2) >> l
        side = z // s % 2
        m = mraw[l].astype(F32)
        mor[l] = jnp.where(side == 0, m, m.T).astype(BF16)

    for l in range(levels):
        arrived(grs.at[:, l], RS_G, l)
    gm[...] = gathered_sum(gs, grs, 0, levels)
    remote(gm, gx, PAIR_R, 0, partner)
    z_to_gather(0)
    arrived(urs, RS_U, 0)
    usum[...] = gathered_sum(us, urs, 0, levels)
    arrived(gx, PAIR_R, 0)
    for k in range(2):
        full = jnp.where(core == k, gm[...], gx[...]).reshape(levels * 8, 2 * rank)
        hi_part = full.astype(BF16)
        low_part = (full - hi_part.astype(F32)).astype(BF16)
        for j in range(2):
            jl = slice(j * rank, (j + 1) * rank)
            ghl[2 * k + j, :levels * 8] = hi_part[:, jl]
            ghl[2 * k + j, levels * 8:] = low_part[:, jl]

    nxt = usum[...].reshape(levels * 8, half)
    for grp, (lo, hi) in ORDER:
        for l, cols in own_group(0, grp, lo, hi):
            both = jnp.dot(ghl[l], cols, preferred_element_type=F32)
            nxt = nxt + (both[:levels * 8] + both[levels * 8:])
    sv[1] = nxt.reshape(levels, 8, half)
    for l in range(levels):
        z_send(1, l)

    for grp, (lo, hi) in ORDER:
        other_group(0, grp, lo, hi)
    first = acc[...] + expand(0, levels)
    for h in range(2):
        hl = slice(h * half, (h + 1) * half)
        xs[:, hl] = (wcol[...] * first[:, hl]).astype(BF16)
    leaf_part(xs)

    z_to_gather(1)
    last = len(ORDER) - 1
    for n, (grp, (lo, hi)) in enumerate(ORDER):
        own_group(1, grp, lo, hi)
        if n >= 1:
            pgrp, (plo, phi) = ORDER[n - 1]
            other_group(1, pgrp, plo, phi)
            acc[...] += expand(plo, phi)
    grp, (lo, hi) = ORDER[last]
    other_group(1, grp, lo, hi)
    out_ref[...] = (acc[...] + expand(lo, hi)).astype(BF16)
    for ref, phase, grp in sent:
        multi_wait(ref, send_sem.at[phase, grp])


def on_device(signal, leaves, bases, couplings, weights):
    rows, width = signal.shape
    levels, _, rank = bases.shape
    count = lax.axis_size("rows")
    scales = [1.0 / math.sqrt(rows * (count >> level + 1) * rank) for level in range(levels)]
    half = width // 2
    vm = pltpu.VMEM
    anyspec = pl.BlockSpec(memory_space=pl.ANY)
    dma = pltpu.SemaphoreType.DMA

    def body(*refs):
        kernel(scales, *refs)

    return pl.pallas_call(
        body,
        name="double_product",
        out_shape=vm((rows, width), BF16),
        in_specs=[anyspec] * 5,
        out_specs=pl.BlockSpec(memory_space=vm),
        scratch_shapes=[
            vm((rows, width), BF16),
            vm((rows, levels * rank), BF16),
            vm((rows, LEAF), BF16),
            vm((levels, rank, rank), BF16),
            vm((levels, rank, rank), BF16),
            vm((rows // 128, 128), F32),
            vm((rows, 128), F32),
            vm((rows, levels * rank), BF16),
            vm((rows, width), BF16),
            vm((rows, width), BF16),
            vm((rows, width), F32),
            vm((levels * rank, width), BF16),
            vm((2, levels, rank, half), F32),
            vm((levels, rank, half), F32),
            vm((levels, rank, half), F32),
            vm((CHIPS - 1, levels, 8, half), F32),
            vm((2 * CHIPS - 1, 8, half), F32),
            vm((2, levels, rank, half), F32),
            vm((levels, rank, half), F32),
            vm((levels, rank, half), F32),
            vm((CHIPS - 1, levels, 8, half), F32),
            vm((2, levels, rank, 2 * rank), F32),
            vm((levels, rank, 2 * rank), F32),
            vm((levels, rank, 2 * rank), F32),
            vm((CHIPS - 1, levels, 8, 2 * rank), F32),
            vm((levels, 8, 2 * rank), F32),
            vm((levels, 8, 2 * rank), F32),
            vm((levels, 2 * levels * 8, rank), BF16),
            vm((levels, 8, half), F32),
            vm((2, levels, 8, half), F32),
            vm((2, PLANES, 8, half), F32),
            vm((2, levels, 8, half), F32),
            vm((2, levels, rank, half), F32),
            vm((2, levels, rank, half), F32),
            dma((16,)),
            dma((13, 4)),
            dma((13, 4)),
            pltpu.SemaphoreType.REGULAR,
        ],
        compiler_params=pltpu.CompilerParams(collective_id=0, has_side_effects=True),
    )(signal, leaves, bases, couplings, weights.reshape(rows // 128, 128))


def solution(mesh):
    in_specs = (P("rows", None), P("rows", None), P(None, "rows", None), P(), P("rows"))
    return jax.shard_map(
        on_device, mesh=mesh, in_specs=in_specs, out_specs=P("rows", None), check_vma=False
    )
```
